256 devices in a mesh: row: 16 (over y, x), col: 8 (over z), depth: 2 (over core).
Axes of the slice: x: 4, y: 4, z: 8, core: 2. Of those that a mesh axis runs over, the one named last changes fastest.
Arguments:
- matrix_columns: float32 [16, 16, 96, 24576], P(None, ('col', 'depth'), None, 'row'), may hold values from -0.0390625 to 0.0390625
- sources: float32 [16, 16, 96, 128], P('row', ('col', 'depth')), may hold values from -6 to 6
Outputs:
- first_image: float32 [16, 16, 96, 128], P('row', ('col', 'depth'))
- second_image: float32 [16, 16, 96, 128], P('row', ('col', 'depth'))
The draws below stay inside these ranges and needn't reach their ends.
All inputs are finite; a program needn't handle non-finite values.
Results may differ from the reference program's by a relative error of at most 0.00011.
Values sent between devices are 32-bit elements; how exact they have to be, the bound alone decides.
No kernel may reach another device: no remote copies, remote signals or barrier semaphores. Data moves between devices by JAX's collectives and lax.ppermute only.
A program may use at most 64 MiB of HBM per device.

```python
import jax
import jax.numpy as jnp
from jax import lax

ORDER = 24576
RHS = 128
PIECE = 96
N_ROW = 16
N_COL = 8
N_DEPTH = 2


def levels(key, shape, shards, least, high):
    gain = 1.0
    for position, parts in shards:
        draws = jax.random.uniform(jax.random.fold_in(jax.random.fold_in(key, 6), position), (parts,), jnp.float32, least / len(shards), high / len(shards))
        gain = gain * jnp.repeat(jnp.exp(draws), shape[position] // parts).reshape((-1,) + (1,) * (len(shape) - 1 - position))
    return gain


def noise(key, dims, width, limit, split=(), held_as=jnp.bfloat16):
    result = jax.random.normal(key, dims, jnp.float32) * width
    if len(split) > 0:
        result = levels(key, dims, split, -0.22, 0.18) * result
    return jnp.clip(result, min=-limit, max=limit).astype(held_as)


def setup_inputs(seed: int = 0) -> dict:
    keys = jax.random.split(jax.random.key(seed), 3)
    matrix_columns = noise(keys[0], (N_ROW, N_COL * N_DEPTH, PIECE, ORDER), ORDER ** -0.5, 0.0390625, ((1, 16), (3, 16)), jnp.float32)
    sources = noise(keys[1], (N_ROW, N_COL * N_DEPTH, PIECE, RHS), 1.0, 6.0, ((0, 16), (1, 16)), jnp.float32)
    return {"matrix_columns": matrix_columns, "sources": sources}


def apply_matrix(matrix_t, vectors):
    return lax.dot_general(matrix_t, vectors, (((0,), (0,)), ((), ())), precision=lax.Precision.HIGHEST, preferred_element_type=jnp.float32)


def reference(matrix_columns, sources):
    matrix_t = matrix_columns.reshape(ORDER, ORDER)
    inputs_flat = sources.reshape(ORDER, RHS)
    first_flat = apply_matrix(matrix_t, inputs_flat)
    second_flat = apply_matrix(matrix_t, first_flat)
    return first_flat.reshape(sources.shape), second_flat.reshape(sources.shape)
```

```python
import functools

import jax
import jax.numpy as jnp
from jax import lax
from jax.experimental import pallas as pl
from jax.experimental.pallas import tpu as pltpu
from jax.sharding import PartitionSpec as P

ROUND = 4
CHUNKS = 3
DIRECT = True
VMEM_LIMIT = 40 * 2**20
SMALL_LIMIT = 10 * 2**20


def split_kernel(slot_ref, matrix_hbm, high_hbm, low_hbm, matrix_ref, high_ref, low_ref, in_sems, out_sems, *, piece):
    width = ROUND * piece
    rounds = matrix_ref.shape[1] // width
    arriving = []
    for i in range(rounds):
        at = pl.ds(i * width, width)
        copy = pltpu.make_async_copy(matrix_hbm.at[:, at], matrix_ref.at[:, at], in_sems.at[i])
        copy.start()
        arriving.append(copy)
    leaving = []
    for i in range(rounds):
        arriving[i].wait()
        turned = matrix_ref[:, i * width : (i + 1) * width].T
        for k in range(ROUND):
            n = i * ROUND + k
            rows = turned[k * piece : (k + 1) * piece]
            high = rows.astype(jnp.bfloat16)
            at = pl.ds(n * piece, piece)
            high_ref[at, :] = high
            low_ref[at, :] = (rows - high.astype(jnp.float32)).astype(jnp.bfloat16)
            there = pl.ds(pl.multiple_of(slot_ref[n] * piece, piece), piece)
            for j, (here, far) in enumerate(((high_ref, high_hbm), (low_ref, low_hbm))):
                copy = pltpu.make_async_copy(here.at[at], far.at[there], out_sems.at[j, n])
                copy.start()
                leaving.append(copy)
    for copy in leaving:
        copy.wait()


def split_matrix(slots, columns, piece):
    depth, rows = columns.shape
    far = pl.BlockSpec(memory_space=pltpu.HBM)
    out = pltpu.HBM((rows, depth), jnp.bfloat16)
    held = pltpu.VMEM((rows, depth), jnp.bfloat16)
    return pl.pallas_call(
        functools.partial(split_kernel, piece=piece),
        in_specs=[pl.BlockSpec(memory_space=pltpu.SMEM), far],
        out_specs=[far, far],
        out_shape=[out, out],
        scratch_shapes=[
            pltpu.VMEM((depth, rows), jnp.float32),
            held,
            held,
            pltpu.SemaphoreType.DMA((rows // (ROUND * piece),)),
            pltpu.SemaphoreType.DMA((2, rows // piece)),
        ],
        compiler_params=pltpu.CompilerParams(vmem_limit_bytes=VMEM_LIMIT),
        name="split_matrix",
    )(slots, pltpu.with_memory_space_constraint(columns, pltpu.HBM))


def halves_of(vectors):
    top = vectors.astype(jnp.bfloat16)
    rest = (vectors - top.astype(jnp.float32)).astype(jnp.bfloat16)
    return top, jnp.concatenate([top, rest], axis=1)


def multiply(high, low, top, both):
    width = top.shape[1]
    main = jnp.dot(high, both, preferred_element_type=jnp.float32)
    small = jnp.dot(low, top, preferred_element_type=jnp.float32)
    return main[:, :width] + (main[:, width:] + small)


def streamed_kernel(high_hbm, low_hbm, vectors_ref, out_ref, high_ref, low_ref, sems, *, start):
    rows = high_ref.shape[0]
    step = rows // CHUNKS
    copies = []
    for k in range(CHUNKS):
        at = pl.ds(k * step, step)
        there = pl.ds(start + k * step, step)
        pair = [
            pltpu.make_async_copy(high_hbm.at[there], high_ref.at[at], sems.at[0, k]),
            pltpu.make_async_copy(low_hbm.at[there], low_ref.at[at], sems.at[1, k]),
        ]
        for copy in pair:
            copy.start()
        copies.append(pair)
    top, both = halves_of(vectors_ref[...])
    for k in range(CHUNKS):
        for copy in copies[k]:
            copy.wait()
        at = pl.ds(k * step, step)
        out_ref[at, :] = multiply(high_ref[at, :], low_ref[at, :], top, both)


def product_streamed(high, low, vectors, half):
    rows, depth = high.shape
    width = vectors.shape[1]
    rows //= 2
    on_chip = pl.BlockSpec(memory_space=pltpu.VMEM)
    far = pl.BlockSpec(memory_space=pltpu.HBM)
    held = pltpu.VMEM((rows, depth), jnp.bfloat16)
    return pl.pallas_call(
        functools.partial(streamed_kernel, start=half * rows),
        in_specs=[far, far, on_chip],
        out_specs=[on_chip, on_chip, on_chip],
        out_shape=[jax.ShapeDtypeStruct((rows, width), jnp.float32), held, held],
        scratch_shapes=[pltpu.SemaphoreType.DMA((2, CHUNKS))],
        compiler_params=pltpu.CompilerParams(vmem_limit_bytes=SMALL_LIMIT),
        name="product_streamed",
    )(*(pltpu.with_memory_space_constraint(m, pltpu.HBM) for m in (high, low)), vectors)


def product_kernel(high_ref, low_ref, vectors_ref, out_ref):
    top, both = halves_of(vectors_ref[...])
    out_ref[...] = multiply(high_ref[...], low_ref[...], top, both)


def product(high, low, vectors):
    on_chip = pl.BlockSpec(memory_space=pltpu.VMEM)
    return pl.pallas_call(
        product_kernel,
        in_specs=[on_chip, on_chip, on_chip],
        out_specs=on_chip,
        out_shape=jax.ShapeDtypeStruct((high.shape[0], vectors.shape[1]), jnp.float32),
        compiler_params=pltpu.CompilerParams(vmem_limit_bytes=SMALL_LIMIT),
        name="product",
    )(high, low, vectors)


def gather_rows(part):
    copies = jnp.broadcast_to(part, (lax.axis_size("row"), *part.shape))
    return lax.all_to_all(copies, "row", split_axis=0, concat_axis=0, tiled=True)


def slots_here(direct):
    ring = lax.axis_size("col")
    core, place = lax.axis_index("depth"), lax.axis_index("col")
    owner = jnp.arange(2 * ring, dtype=jnp.int32)
    chip, owner_core = owner // 2, owner % 2
    if not direct:
        return jnp.where(owner_core == core, 0, ring) + chip
    ahead = jnp.remainder(chip - place, ring)
    half = ring // 2
    before = ahead > half
    hops = jnp.where(before, ring - ahead, ahead)
    shared = (ahead == 0) | (ahead == half)
    handler = jnp.where(shared, owner_core, before.astype(jnp.int32))
    slot = jnp.where(shared, jnp.where(ahead == 0, ring - 1, ring - 2), 2 * (hops - 1) + owner_core)
    return (jnp.where(handler == core, 0, ring) + slot).astype(jnp.int32)


SWAP = [(0, 1), (1, 0)]


def to_owners(ours, theirs, core_row, piece):
    width = ours.shape[-1]
    ring = lax.axis_size("col")
    received = lax.ppermute(theirs, "depth", SWAP)
    summed = (ours + received).reshape(-1, piece, width)
    if not DIRECT:
        tiles = lax.all_to_all(summed, "col", 0, 0, tiled=True)
        return jnp.sum(tiles, axis=0)
    axes = ("col", "depth")

    def pairs(hops):
        return [(2 * z + c, 2 * ((z + (1 - 2 * c) * hops) % ring) + c) for z in range(ring) for c in range(2)]

    half = ring // 2
    arrived = []
    for hops in range(1, half):
        arrived.append(lax.ppermute(summed[2 * (hops - 1) : 2 * hops], axes, pairs(hops)))
    opposite = lax.ppermute(summed[ring - 2], axes, pairs(half))
    both = sum(arrived[1:], arrived[0])
    first_core = core_row == 0
    give = jnp.where(first_core, both[1], both[0])
    keep = jnp.where(first_core, both[0], both[1])
    last = lax.ppermute(give, "depth", SWAP)
    return summed[ring - 1] + opposite + keep + last


def body(matrix_columns, sources):
    rows_here = matrix_columns.shape[3]
    piece, width = sources.shape[2:]
    gathered = gather_rows(sources.reshape(piece, width)).reshape(-1, width)
    core_row = lax.optimization_barrier(jnp.broadcast_to(lax.axis_index("depth"), (1, width)))
    high, low = split_matrix(slots_here(DIRECT), matrix_columns.reshape(-1, rows_here), piece)
    theirs, their_high, their_low = product_streamed(high, low, gathered, 1)
    ours, our_high, our_low = product_streamed(high, low, gathered, 0)
    first = to_owners(ours, theirs, core_row, piece)
    gathered = gather_rows(first).reshape(-1, width)
    theirs = product(their_high, their_low, gathered)
    ours = product(our_high, our_low, gathered)
    second = to_owners(ours, theirs, core_row, piece)
    return first.reshape(sources.shape), second.reshape(sources.shape)


def solution(mesh):
    in_specs = (P(None, ("col", "depth"), None, "row"), P("row", ("col", "depth"), None, None))
    out_specs = (P("row", ("col", "depth"), None, None), P("row", ("col", "depth"), None, None))
    return jax.shard_map(body, mesh=mesh, in_specs=in_specs, out_specs=out_specs, check_vma=False)
```

```python
import functools

import jax
import jax.numpy as jnp
from jax import lax
from jax.experimental import pallas as pl
from jax.experimental.pallas import tpu as pltpu
from jax.sharding import PartitionSpec as P

ROUND = 4
SIDE = 4
SHIFTS = (0, 1, 3, 2)
PARTS = 1
VMEM_LIMIT = 40 * 2**20
SMALL_LIMIT = 10 * 2**20


def split_kernel(slot_ref, source_ref, matrix_hbm, high_ref, low_ref, matrix_ref, sems, *, piece, first):
    count = matrix_ref.shape[0] // piece
    owners = matrix_ref.shape[1] // piece
    width = ROUND * piece
    rounds = [(i, j) for i in range(count // ROUND) for j in range(owners // ROUND)]
    arriving = {}
    for i, j in rounds:
        across = pl.ds(j * width, width)
        for n in range(i * ROUND, (i + 1) * ROUND):
            there = pl.ds(pl.multiple_of(source_ref[first + n] * piece, piece), piece)
            copy = pltpu.make_async_copy(
                matrix_hbm.at[there, across], matrix_ref.at[pl.ds(n * piece, piece), across], sems.at[n, j]
            )
            copy.start()
            arriving[n, j] = copy
    for i, j in rounds:
        for n in range(i * ROUND, (i + 1) * ROUND):
            arriving[n, j].wait()
        cols = slice(i * width, (i + 1) * width)
        turned = matrix_ref[cols, j * width : (j + 1) * width].T
        for k in range(ROUND):
            rows = turned[k * piece : (k + 1) * piece]
            high = rows.astype(jnp.bfloat16)
            at = pl.ds(pl.multiple_of(slot_ref[j * ROUND + k] * piece, piece), piece)
            high_ref[at, cols] = high
            low_ref[at, cols] = (rows - high.astype(jnp.float32)).astype(jnp.bfloat16)


def split_matrix(slots, sources, columns, piece, first, count):
    rows = columns.shape[1]
    depth = count * piece
    scalars = pl.BlockSpec(memory_space=pltpu.SMEM)
    on_chip = pl.BlockSpec(memory_space=pltpu.VMEM)
    out = pltpu.VMEM((rows, depth), jnp.bfloat16)
    return pl.pallas_call(
        functools.partial(split_kernel, piece=piece, first=first),
        in_specs=[scalars, scalars, pl.BlockSpec(memory_space=pltpu.HBM)],
        out_specs=[on_chip, on_chip],
        out_shape=[out, out],
        scratch_shapes=[pltpu.VMEM((depth, rows), jnp.float32), pltpu.SemaphoreType.DMA((count, rows // (ROUND * piece)))],
        compiler_params=pltpu.CompilerParams(vmem_limit_bytes=VMEM_LIMIT),
        name="split_matrix",
    )(slots, sources, pltpu.with_memory_space_constraint(columns, pltpu.HBM))


def product_kernel(*refs, half, parts):
    matrix, vectors, out_ref = refs[: 2 * parts], refs[2 * parts : -1], refs[-1]
    rows, width = out_ref.shape
    at = pl.ds(half * rows, rows)
    each = len(vectors) // parts
    total = None
    for n in range(parts):
        part = jnp.concatenate([v[...] for v in vectors[n * each : (n + 1) * each]], axis=0)
        top = part.astype(jnp.bfloat16)
        rest = (part - top.astype(jnp.float32)).astype(jnp.bfloat16)
        both = jnp.concatenate([top, rest], axis=1)
        main = jnp.dot(matrix[2 * n][at, :], both, preferred_element_type=jnp.float32)
        small = jnp.dot(matrix[2 * n + 1][at, :], top, preferred_element_type=jnp.float32)
        part_sum = main[:, :width] + (main[:, width:] + small)
        total = part_sum if total is None else total + part_sum
    out_ref[...] = total


def product(matrix, vectors, half):
    rows = matrix[0].shape[0] // 2
    on_chip = pl.BlockSpec(memory_space=pltpu.VMEM)
    return pl.pallas_call(
        functools.partial(product_kernel, half=half, parts=len(matrix) // 2),
        in_specs=[on_chip] * (len(matrix) + len(vectors)),
        out_specs=on_chip,
        out_shape=jax.ShapeDtypeStruct((rows, vectors[0].shape[1]), jnp.float32),
        compiler_params=pltpu.CompilerParams(vmem_limit_bytes=SMALL_LIMIT),
        name="product",
    )(*matrix, *vectors)


def gather_pairs(first, shift):
    pairs = []
    for y in range(SIDE):
        for x in range(SIDE):
            for core in range(2):
                along_x = (core == 0) == first
                to = (y, (x + shift) % SIDE) if along_x else ((y + shift) % SIDE, x)
                pairs.append(((y * SIDE + x) * 2 + core, (to[0] * SIDE + to[1]) * 2 + core))
    return pairs


def first_round(part):
    return [lax.ppermute(part, ("row", "depth"), gather_pairs(True, shift)) for shift in SHIFTS[1:]]


def second_round(line):
    return [line] + [lax.ppermute(line, ("row", "depth"), gather_pairs(False, shift)) for shift in SHIFTS[1:]]


def sources_here():
    row, core = lax.axis_index("row"), lax.axis_index("depth")
    row, core = row.astype(jnp.uint32), core.astype(jnp.int32)
    y, x = (row // SIDE).astype(jnp.int32), (row % SIDE).astype(jnp.int32)
    place = jnp.arange(SIDE * SIDE, dtype=jnp.int32)
    inner, outer = place % SIDE, place // SIDE
    inner, outer = inner ^ (inner >> 1), outer ^ (outer >> 1)
    y = (y - jnp.where(core == 0, outer, inner)) & (SIDE - 1)
    x = (x - jnp.where(core == 0, inner, outer)) & (SIDE - 1)
    return (y * SIDE + x).astype(jnp.int32)


def slots_here():
    ring = lax.axis_size("col")
    core, place = lax.axis_index("depth"), lax.axis_index("col")
    owner = jnp.arange(2 * ring, dtype=jnp.int32)
    chip, owner_core = owner // 2, owner % 2
    ahead = jnp.remainder(chip - place, ring)
    half = ring // 2
    before = ahead > half
    hops = jnp.where(before, ring - ahead, ahead)
    shared = (ahead == 0) | (ahead == half)
    handler = jnp.where(shared, owner_core, before.astype(jnp.int32))
    slot = jnp.where(shared, jnp.where(ahead == 0, ring - 1, ring - 2), 2 * (hops - 1) + owner_core)
    return (jnp.where(handler == core, 0, ring) + slot).astype(jnp.int32)


SWAP = [(0, 1), (1, 0)]


def to_owners(ours, theirs, core_row, piece):
    width = ours.shape[-1]
    ring = lax.axis_size("col")
    received = lax.ppermute(theirs, "depth", SWAP)
    summed = (ours + received).reshape(-1, piece, width)
    axes = ("col", "depth")

    def pairs(hops):
        return [(2 * z + c, 2 * ((z + (1 - 2 * c) * hops) % ring) + c) for z in range(ring) for c in range(2)]

    half = ring // 2
    arrived = []
    for hops in range(1, half):
        arrived.append(lax.ppermute(summed[2 * (hops - 1) : 2 * hops], axes, pairs(hops)))
    opposite = lax.ppermute(summed[ring - 2], axes, pairs(half))
    both = sum(arrived[1:], arrived[0])
    first_core = core_row == 0
    give = jnp.where(first_core, both[1], both[0])
    keep = jnp.where(first_core, both[0], both[1])
    last = lax.ppermute(give, "depth", SWAP)
    return summed[ring - 1] + opposite + keep + last


def body(matrix_columns, sources):
    rows_here = matrix_columns.shape[3]
    piece, width = sources.shape[2:]
    columns = matrix_columns.reshape(-1, rows_here)
    core_row = jnp.broadcast_to(lax.axis_index("depth"), (1, width))
    slots, order, core_row = lax.optimization_barrier((slots_here(), sources_here(), core_row))
    part = sources.reshape(piece, width)
    others = first_round(part)
    count = columns.shape[0] // piece // PARTS
    matrix = []
    results = []
    for step in range(2):
        gathered = second_round(jnp.concatenate([part] + list(others), axis=0))
        for n in range(len(matrix) // 2, PARTS):
            matrix = matrix + list(split_matrix(slots, order, columns, piece, n * count, count))
        theirs = product(matrix, gathered, 1)
        ours = product(matrix, gathered, 0)
        part = to_owners(ours, theirs, core_row, piece)
        results.append(part)
        if step == 0:
            others = first_round(part)
    return tuple(r.reshape(sources.shape) for r in results)


def solution(mesh):
    in_specs = (P(None, ("col", "depth"), None, "row"), P("row", ("col", "depth"), None, None))
    out_specs = (P("row", ("col", "depth"), None, None), P("row", ("col", "depth"), None, None))
    return jax.shard_map(body, mesh=mesh, in_specs=in_specs, out_specs=out_specs, check_vma=False)
```

```python
import functools

import jax
import jax.numpy as jnp
from jax import lax
from jax.experimental import pallas as pl
from jax.experimental.pallas import tpu as pltpu
from jax.sharding import PartitionSpec as P

ROUND = 4
SIDE = 4
SHIFTS = (0, 1, 3, 2)
PARTS = 1
VMEM_LIMIT = 40 * 2**20
SMALL_LIMIT = 10 * 2**20


def split_kernel(slot_ref, source_ref, matrix_hbm, high_ref, low_ref, matrix_ref, sems, *, piece, first):
    count = matrix_ref.shape[0] // piece
    owners = matrix_ref.shape[1] // piece
    width = ROUND * piece
    rounds = [(i, j) for i in range(count // ROUND) for j in range(owners // ROUND)]
    arriving = []
    for n in range(count):
        there = pl.ds(pl.multiple_of(source_ref[first + n] * piece, piece), piece)
        copy = pltpu.make_async_copy(matrix_hbm.at[there, :], matrix_ref.at[pl.ds(n * piece, piece), :], sems.at[n])
        copy.start()
        arriving.append(copy)
    for i, j in rounds:
        if j == 0:
            for copy in arriving[i * ROUND : (i + 1) * ROUND]:
                copy.wait()
        cols = slice(i * width, (i + 1) * width)
        turned = matrix_ref[cols, j * width : (j + 1) * width].T
        for k in range(ROUND):
            rows = turned[k * piece : (k + 1) * piece]
            high = rows.astype(jnp.bfloat16)
            at = pl.ds(pl.multiple_of(slot_ref[j * ROUND + k] * piece, piece), piece)
            high_ref[at, cols] = high
            low_ref[at, cols] = (rows - high.astype(jnp.float32)).astype(jnp.bfloat16)


def split_matrix(slots, sources, columns, piece, first, count):
    rows = columns.shape[1]
    depth = count * piece
    scalars = pl.BlockSpec(memory_space=pltpu.SMEM)
    on_chip = pl.BlockSpec(memory_space=pltpu.VMEM)
    out = pltpu.VMEM((rows, depth), jnp.bfloat16)
    return pl.pallas_call(
        functools.partial(split_kernel, piece=piece, first=first),
        in_specs=[scalars, scalars, pl.BlockSpec(memory_space=pltpu.HBM)],
        out_specs=[on_chip, on_chip],
        out_shape=[out, out],
        scratch_shapes=[pltpu.VMEM((depth, rows), jnp.float32), pltpu.SemaphoreType.DMA((count,))],
        compiler_params=pltpu.CompilerParams(vmem_limit_bytes=VMEM_LIMIT),
        name="split_matrix",
    )(slots, sources, pltpu.with_memory_space_constraint(columns, pltpu.HBM))


def hold_kernel(part_ref, held_ref):
    held_ref[...] = part_ref[...]


def bundle_kernel(*refs):
    rows = refs[0].shape[0]
    for n, ref in enumerate(refs[:-1]):
        refs[-1][n * rows : (n + 1) * rows, :] = ref[...]


def on_chip_call(kernel, out, name, *operands):
    on_chip = pl.BlockSpec(memory_space=pltpu.VMEM)
    return pl.pallas_call(kernel, in_specs=[on_chip] * len(operands), out_specs=on_chip, out_shape=out, name=name, compiler_params=pltpu.CompilerParams(vmem_limit_bytes=2**20))(*operands)


def bundle(part, others):
    rows, width = others[0].shape
    out = jax.ShapeDtypeStruct((rows * (1 + len(others)), width), others[0].dtype)
    return on_chip_call(bundle_kernel, out, "bundle", part, *others)


def product_kernel(*refs, half, parts):
    matrix, vectors, out_ref = refs[: 2 * parts], refs[2 * parts : -1], refs[-1]
    rows, width = out_ref.shape
    at = pl.ds(half * rows, rows)
    each = len(vectors) // parts
    total = None
    for n in range(parts):
        part = jnp.concatenate([v[...] for v in vectors[n * each : (n + 1) * each]], axis=0)
        top = part.astype(jnp.bfloat16)
        rest = (part - top.astype(jnp.float32)).astype(jnp.bfloat16)
        both = jnp.concatenate([top, rest], axis=1)
        main = jnp.dot(matrix[2 * n][at, :], both, preferred_element_type=jnp.float32)
        small = jnp.dot(matrix[2 * n + 1][at, :], top, preferred_element_type=jnp.float32)
        part_sum = main[:, :width] + (main[:, width:] + small)
        total = part_sum if total is None else total + part_sum
    out_ref[...] = total


def product(matrix, vectors, half):
    rows = matrix[0].shape[0] // 2
    on_chip = pl.BlockSpec(memory_space=pltpu.VMEM)
    return pl.pallas_call(
        functools.partial(product_kernel, half=half, parts=len(matrix) // 2),
        in_specs=[on_chip] * (len(matrix) + len(vectors)),
        out_specs=on_chip,
        out_shape=jax.ShapeDtypeStruct((rows, vectors[0].shape[1]), jnp.float32),
        compiler_params=pltpu.CompilerParams(vmem_limit_bytes=SMALL_LIMIT),
        name="product",
    )(*matrix, *vectors)


def gather_pairs(first, shift):
    pairs = []
    for y in range(SIDE):
        for x in range(SIDE):
            for core in range(2):
                along_x = (core == 0) == first
                to = (y, (x + shift) % SIDE) if along_x else ((y + shift) % SIDE, x)
                pairs.append(((y * SIDE + x) * 2 + core, (to[0] * SIDE + to[1]) * 2 + core))
    return pairs


def first_round(part):
    return [lax.ppermute(part, ("row", "depth"), gather_pairs(True, shift)) for shift in SHIFTS[1:]]


def second_round(line):
    return [line] + [lax.ppermute(line, ("row", "depth"), gather_pairs(False, shift)) for shift in SHIFTS[1:]]


def sources_here():
    row, core = lax.axis_index("row"), lax.axis_index("depth")
    row, core = row.astype(jnp.uint32), core.astype(jnp.int32)
    y, x = (row // SIDE).astype(jnp.int32), (row % SIDE).astype(jnp.int32)
    place = jnp.arange(SIDE * SIDE, dtype=jnp.int32)
    inner, outer = place % SIDE, place // SIDE
    inner, outer = inner ^ (inner >> 1), outer ^ (outer >> 1)
    y = (y - jnp.where(core == 0, outer, inner)) & (SIDE - 1)
    x = (x - jnp.where(core == 0, inner, outer)) & (SIDE - 1)
    return (y * SIDE + x).astype(jnp.int32)


def slots_here():
    ring = lax.axis_size("col")
    core, place = lax.axis_index("depth"), lax.axis_index("col")
    owner = jnp.arange(2 * ring, dtype=jnp.int32)
    chip, owner_core = owner // 2, owner % 2
    ahead = jnp.remainder(chip - place, ring)
    half = ring // 2
    before = ahead > half
    hops = jnp.where(before, ring - ahead, ahead)
    shared = (ahead == 0) | (ahead == half)
    handler = jnp.where(shared, owner_core, before.astype(jnp.int32))
    slot = jnp.where(shared, jnp.where(ahead == 0, ring - 1, ring - 2), 2 * (hops - 1) + owner_core)
    return (jnp.where(handler == core, 0, ring) + slot).astype(jnp.int32)


SWAP = [(0, 1), (1, 0)]


def to_owners(ours, theirs, core_row, piece):
    width = ours.shape[-1]
    ring = lax.axis_size("col")
    received = lax.ppermute(theirs, "depth", SWAP)
    summed = (ours + received).reshape(-1, piece, width)
    axes = ("col", "depth")

    def pairs(hops):
        return [(2 * z + c, 2 * ((z + (1 - 2 * c) * hops) % ring) + c) for z in range(ring) for c in range(2)]

    half = ring // 2
    arrived = []
    for hops in range(1, half):
        arrived.append(lax.ppermute(summed[2 * (hops - 1) : 2 * hops], axes, pairs(hops)))
    opposite = lax.ppermute(summed[ring - 2], axes, pairs(half))
    both = sum(arrived[1:], arrived[0])
    first_core = core_row == 0
    give = jnp.where(first_core, both[1], both[0])
    keep = jnp.where(first_core, both[0], both[1])
    last = lax.ppermute(give, "depth", SWAP)
    return summed[ring - 1] + opposite + keep + last


def body(matrix_columns, sources):
    rows_here = matrix_columns.shape[3]
    piece, width = sources.shape[2:]
    columns = matrix_columns.reshape(-1, rows_here)
    core_row = jnp.broadcast_to(lax.axis_index("depth"), (1, width))
    slots, order, core_row = lax.optimization_barrier((slots_here(), sources_here(), core_row))
    part = sources.reshape(piece, width)
    others = first_round(part)
    part = on_chip_call(hold_kernel, pltpu.VMEM(part.shape, part.dtype), "hold", part)
    count = columns.shape[0] // piece // PARTS
    matrix = []
    results = []
    for step in range(2):
        gathered = second_round(bundle(part, others))
        for n in range(len(matrix) // 2, PARTS):
            matrix = matrix + list(split_matrix(slots, order, columns, piece, n * count, count))
        theirs = product(matrix, gathered, 1)
        ours = product(matrix, gathered, 0)
        part = to_owners(ours, theirs, core_row, piece)
        results.append(part)
        if step == 0:
            others = first_round(part)
    return tuple(r.reshape(sources.shape) for r in results)


def solution(mesh):
    in_specs = (P(None, ("col", "depth"), None, "row"), P("row", ("col", "depth"), None, None))
    out_specs = (P("row", ("col", "depth"), None, None), P("row", ("col", "depth"), None, None))
    return jax.shard_map(body, mesh=mesh, in_specs=in_specs, out_specs=out_specs, check_vma=False)
```

```python
import functools

import jax
import jax.numpy as jnp
from jax import lax
from jax.experimental import pallas as pl
from jax.experimental.pallas import tpu as pltpu
from jax.sharding import PartitionSpec as P

ROUND = 4
SIDE = 4
SHIFTS = (0, 1, 3, 2)
PARTS = 1
VMEM_LIMIT = 40 * 2**20
SMALL_LIMIT = 10 * 2**20


def split_kernel(slot_ref, source_ref, matrix_hbm, parts_ref, matrix_ref, sems, *, piece, first):
    count = matrix_ref.shape[0] // piece
    owners = matrix_ref.shape[1] // piece
    width = ROUND * piece
    rounds = [(i, j) for i in range(count // ROUND) for j in range(owners // ROUND)]
    arriving = []
    for n in range(count):
        there = pl.ds(pl.multiple_of(source_ref[first + n] * piece, piece), piece)
        copy = pltpu.make_async_copy(matrix_hbm.at[there, :], matrix_ref.at[pl.ds(n * piece, piece), :], sems.at[n])
        copy.start()
        arriving.append(copy)
    for i, j in rounds:
        if j == 0:
            for copy in arriving[i * ROUND : (i + 1) * ROUND]:
                copy.wait()
        cols = slice(i * width, (i + 1) * width)
        turned = matrix_ref[cols, j * width : (j + 1) * width].T
        for k in range(ROUND):
            rows = turned[k * piece : (k + 1) * piece]
            high = rows.astype(jnp.bfloat16)
            start = pl.multiple_of(slot_ref[j * ROUND + k] * piece, piece)
            parts_ref[pl.ds(start, piece), cols] = high
            below = pl.multiple_of(start + owners * piece // 2, piece)
            parts_ref[pl.ds(below, piece), cols] = (rows - high.astype(jnp.float32)).astype(jnp.bfloat16)


def split_matrix(slots, sources, columns, piece, first, count):
    rows = columns.shape[1]
    depth = count * piece
    scalars = pl.BlockSpec(memory_space=pltpu.SMEM)
    on_chip = pl.BlockSpec(memory_space=pltpu.VMEM)
    out = pltpu.VMEM((2 * rows, depth), jnp.bfloat16)
    return pl.pallas_call(
        functools.partial(split_kernel, piece=piece, first=first),
        in_specs=[scalars, scalars, pl.BlockSpec(memory_space=pltpu.HBM)],
        out_specs=[on_chip],
        out_shape=[out],
        scratch_shapes=[pltpu.VMEM((depth, rows), jnp.float32), pltpu.SemaphoreType.DMA((count,))],
        compiler_params=pltpu.CompilerParams(vmem_limit_bytes=VMEM_LIMIT),
        name="split_matrix",
    )(slots, sources, pltpu.with_memory_space_constraint(columns, pltpu.HBM))


def hold_kernel(part_ref, held_ref):
    held_ref[...] = part_ref[...]


def bundle_kernel(*refs):
    rows = refs[0].shape[0]
    for n, ref in enumerate(refs[:-1]):
        refs[-1][n * rows : (n + 1) * rows, :] = ref[...]


def on_chip_call(kernel, out, name, *operands):
    on_chip = pl.BlockSpec(memory_space=pltpu.VMEM)
    return pl.pallas_call(kernel, in_specs=[on_chip] * len(operands), out_specs=on_chip, out_shape=out, name=name, compiler_params=pltpu.CompilerParams(vmem_limit_bytes=2**20))(*operands)


def bundle(part, others):
    rows, width = others[0].shape
    out = jax.ShapeDtypeStruct((rows * (1 + len(others)), width), others[0].dtype)
    return on_chip_call(bundle_kernel, out, "bundle", part, *others)


def product_kernel(*refs, half, parts):
    matrix, vectors, out_ref = refs[:parts], refs[parts:-1], refs[-1]
    rows, width = out_ref.shape
    at = pl.ds(half * 2 * rows, 2 * rows)
    each = len(vectors) // parts
    total = None
    for n in range(parts):
        part = jnp.concatenate([v[...] for v in vectors[n * each : (n + 1) * each]], axis=0)
        top = part.astype(jnp.bfloat16)
        rest = (part - top.astype(jnp.float32)).astype(jnp.bfloat16)
        both = jnp.concatenate([top, rest], axis=1)
        four = jnp.dot(matrix[n][at, :], both, preferred_element_type=jnp.float32)
        main, small = four[:rows], four[rows:]
        part_sum = main[:, :width] + (main[:, width:] + (small[:, :width] + small[:, width:]))
        total = part_sum if total is None else total + part_sum
    out_ref[...] = total


def product(matrix, vectors, half):
    rows = matrix[0].shape[0] // 4
    on_chip = pl.BlockSpec(memory_space=pltpu.VMEM)
    return pl.pallas_call(
        functools.partial(product_kernel, half=half, parts=len(matrix)),
        in_specs=[on_chip] * (len(matrix) + len(vectors)),
        out_specs=on_chip,
        out_shape=jax.ShapeDtypeStruct((rows, vectors[0].shape[1]), jnp.float32),
        compiler_params=pltpu.CompilerParams(vmem_limit_bytes=SMALL_LIMIT),
        name="product",
    )(*matrix, *vectors)


def gather_pairs(first, shift):
    pairs = []
    for y in range(SIDE):
        for x in range(SIDE):
            for core in range(2):
                along_x = (core == 0) == first
                to = (y, (x + shift) % SIDE) if along_x else ((y + shift) % SIDE, x)
                pairs.append(((y * SIDE + x) * 2 + core, (to[0] * SIDE + to[1]) * 2 + core))
    return pairs


def first_round(part):
    return [lax.ppermute(part, ("row", "depth"), gather_pairs(True, shift)) for shift in SHIFTS[1:]]


def second_round(line):
    return [line] + [lax.ppermute(line, ("row", "depth"), gather_pairs(False, shift)) for shift in SHIFTS[1:]]


def sources_here():
    row, core = lax.axis_index("row"), lax.axis_index("depth")
    row, core = row.astype(jnp.uint32), core.astype(jnp.int32)
    y, x = (row // SIDE).astype(jnp.int32), (row % SIDE).astype(jnp.int32)
    place = jnp.arange(SIDE * SIDE, dtype=jnp.int32)
    inner, outer = place % SIDE, place // SIDE
    inner, outer = inner ^ (inner >> 1), outer ^ (outer >> 1)
    y = (y - jnp.where(core == 0, outer, inner)) & (SIDE - 1)
    x = (x - jnp.where(core == 0, inner, outer)) & (SIDE - 1)
    return (y * SIDE + x).astype(jnp.int32)


def slots_here():
    ring = lax.axis_size("col")
    core, place = lax.axis_index("depth"), lax.axis_index("col")
    owner = jnp.arange(2 * ring, dtype=jnp.int32)
    chip, owner_core = owner // 2, owner % 2
    ahead = jnp.remainder(chip - place, ring)
    half = ring // 2
    before = ahead > half
    hops = jnp.where(before, ring - ahead, ahead)
    shared = (ahead == 0) | (ahead == half)
    handler = jnp.where(shared, owner_core, before.astype(jnp.int32))
    slot = jnp.where(shared, jnp.where(ahead == 0, ring - 1, ring - 2), 2 * (hops - 1) + owner_core)
    return (jnp.where(handler == core, 0, 2 * ring) + slot).astype(jnp.int32)


SWAP = [(0, 1), (1, 0)]


def to_owners(ours, theirs, core_row, piece):
    width = ours.shape[-1]
    ring = lax.axis_size("col")
    received = lax.ppermute(theirs, "depth", SWAP)
    summed = (ours + received).reshape(-1, piece, width)
    axes = ("col", "depth")

    def pairs(hops):
        return [(2 * z + c, 2 * ((z + (1 - 2 * c) * hops) % ring) + c) for z in range(ring) for c in range(2)]

    half = ring // 2
    arrived = []
    for hops in range(1, half):
        arrived.append(lax.ppermute(summed[2 * (hops - 1) : 2 * hops], axes, pairs(hops)))
    opposite = lax.ppermute(summed[ring - 2], axes, pairs(half))
    both = sum(arrived[1:], arrived[0])
    first_core = core_row == 0
    give = jnp.where(first_core, both[1], both[0])
    keep = jnp.where(first_core, both[0], both[1])
    last = lax.ppermute(give, "depth", SWAP)
    return summed[ring - 1] + opposite + keep + last


def body(matrix_columns, sources):
    rows_here = matrix_columns.shape[3]
    piece, width = sources.shape[2:]
    columns = matrix_columns.reshape(-1, rows_here)
    core_row = jnp.broadcast_to(lax.axis_index("depth"), (1, width))
    slots, order, core_row = lax.optimization_barrier((slots_here(), sources_here(), core_row))
    part = sources.reshape(piece, width)
    others = first_round(part)
    part = on_chip_call(hold_kernel, pltpu.VMEM(part.shape, part.dtype), "hold", part)
    count = columns.shape[0] // piece // PARTS
    matrix = []
    results = []
    for step in range(2):
        gathered = second_round(bundle(part, others))
        for n in range(len(matrix), PARTS):
            matrix = matrix + list(split_matrix(slots, order, columns, piece, n * count, count))
        theirs = product(matrix, gathered, 1)
        ours = product(matrix, gathered, 0)
        part = to_owners(ours, theirs, core_row, piece)
        results.append(part)
        if step == 0:
            others = first_round(part)
    return tuple(r.reshape(sources.shape) for r in results)


def solution(mesh):
    in_specs = (P(None, ("col", "depth"), None, "row"), P("row", ("col", "depth"), None, None))
    out_specs = (P("row", ("col", "depth"), None, None), P("row", ("col", "depth"), None, None))
    return jax.shard_map(body, mesh=mesh, in_specs=in_specs, out_specs=out_specs, check_vma=False)
```
